32 devices in a mesh: grp: 2 (over y), ctx: 4 (over z), tp: 4 (over x, core).
Axes of the slice: x: 2, y: 2, z: 4, core: 2. Of those that a mesh axis runs over, the one named last changes fastest.
Arguments:
- residual: bfloat16 [1024, 7168], P(('grp', 'ctx'), 'tp'), parts along dimension 0, may hold values from -20 to 20
- latent: bfloat16 [576, 1024], P(None, ('grp', 'ctx')), parts along dimension 1, may hold values from -4 to 4
- queries: bfloat16 [1024, 36864], P(('grp', 'ctx'), 'tp'), parts along dimension 0, may hold values from -32 to 32
- lengths: int32 [8], P('grp'), parts along dimension 0, may hold values from 1 to 384, 512 in all
- value_weight: bfloat16 [512, 8192], P(None, 'tp'), may hold values from -1 to 1
- output_weight: bfloat16 [8192, 7168], P('ctx', 'tp'), may hold values from -0.0625 to 0.0625
- norm_gain: float32 [7168], P('tp'), may hold values from 0.1 to 1.9
- gate_weight: bfloat16 [7168, 10240], P('tp', 'ctx'), may hold values from -0.0625 to 0.0625
- up_weight: bfloat16 [7168, 10240], P('tp', 'ctx'), may hold values from -0.0625 to 0.0625
- down_weight: bfloat16 [10240, 7168], P('ctx', 'tp'), may hold values from -0.0625 to 0.0625
Outputs:
- attended: bfloat16 [1024, 7168], P(('grp', 'ctx'), 'tp'), parts along dimension 0
- layer_out: bfloat16 [1024, 7168], P(('grp', 'ctx'), 'tp'), parts along dimension 0
The draws below stay inside these ranges and needn't reach their ends.
There are 2 independent parts, one for each index of `grp`. The reference program is written for one: setup_inputs(seed, part) draws one part's arguments, and reference() takes and returns one part's arrays. A program takes and returns all parts, laid end to end along the dimension named above; an argument that names none is the same for every part. Nothing has to cross between parts.
Inputs may be any that keep to these rules, and one draw needn't show every extreme that they name: The 4 traces fill the sequence in order and their lengths sum to 512.
All inputs are finite; a program needn't handle non-finite values.
Results may differ from the reference program's by a relative error of at most 0.02.
Values may be sent and summed in bfloat16 or wider, within the bound.
A program may use at most 128 MiB of HBM per device.

```python
import math
import jax
import jax.numpy as jnp
import numpy as np
from jax import lax

D = 7168
HEADS = 64
LAT = 512
ROPE = 64
VHEAD = 128
FF = 10240
SEQS = 4
TOKENS = 512
DGROUP = 1792
HGROUP = 2048
FGROUP = 2560
N_CTX = 4
N_TP = 4


def latent_base(key):
    width_all = LAT + ROPE
    base = jnp.clip(jax.random.normal(jax.random.fold_in(key, 11), (width_all, TOKENS), jnp.float32), -4.0, 4.0)
    return base


def draw_latent(key, part):
    return latent_base(key).astype(jnp.bfloat16)


def draw_queries(key, part):
    width_all = LAT + ROPE
    base = 0.8 * jnp.clip(jax.random.normal(jax.random.fold_in(key, 13), (TOKENS, HEADS, width_all), jnp.float32), -4.0, 4.0)
    return base.reshape(TOKENS, HEADS * width_all).astype(jnp.bfloat16)


def draw_residual(key, part):
    row_scale = jnp.exp(jax.random.uniform(jax.random.fold_in(key, 21), (TOKENS, 1), jnp.float32, jnp.log(0.2), jnp.log(2.0)))
    jitter = jnp.exp(jax.random.uniform(jax.random.fold_in(key, 22), (1, D), jnp.float32, jnp.log(0.7), jnp.log(1.4)))
    ramp = jnp.arange(D, dtype=jnp.float32)[None, :] / (D - 1)
    col_scale = 3.0 ** ramp * jitter / 1.9
    noise_part = jnp.clip(jax.random.normal(jax.random.fold_in(key, 23), (TOKENS, D), jnp.float32), -4.0, 4.0)
    value_all = row_scale * noise_part * col_scale
    return jnp.clip(value_all, -20.0, 20.0).astype(jnp.bfloat16)


def shard_levels(key, shape, pieces, least, high):
    level = 1.0
    for dim, blocks in pieces:
        heights = jax.random.uniform(jax.random.fold_in(jax.random.fold_in(key, 6), dim), (blocks,), jnp.float32, least / len(pieces), high / len(pieces))
        level = level * jnp.repeat(jnp.exp(heights), shape[dim] // blocks).reshape((-1,) + (1,) * (len(shape) - 1 - dim))
    return level


def length_profile(count, total, bound, skew):
    loads = [(1 << 20) // math.isqrt(rank ** skew) + 1 for rank in range(2, count + 1)]
    surplus, given = total - bound - (count - 1), [1] * (count - 1)
    while surplus > 0:
        candidates = [i for i in range(count - 1) if given[i] < bound]
        mass, remaining = sum([loads[i] for i in candidates]), surplus
        for i in candidates:
            more = min(bound - given[i], max(1, remaining * loads[i] // mass), surplus)
            given[i] = given[i] + more
            surplus = surplus - more
    return np.array([bound] + given)


def ragged_sizes(rng, number_of, total, bound, slope):
    if number_of == 2:
        one = jax.random.randint(rng, (), max(1, total - bound), min(bound, total - 1) + 1)
        return jnp.stack([one, total - one])
    sizes = jnp.asarray(length_profile(number_of, total, bound, slope), jnp.int32)
    twos = (number_of - 1) // 2
    source_of, taker = sizes[1:1 + 2 * twos:2], sizes[2:2 + 2 * twos:2]
    margin = jnp.minimum(source_of - 1, bound - taker)
    passed = jax.random.randint(jax.random.fold_in(rng, 1), (twos,), 0, 1 << 20) % (margin + 1)
    sizes = sizes.at[1:1 + 2 * twos:2].set(source_of - passed).at[2:2 + 2 * twos:2].set(taker + passed)
    return sizes[jax.random.permutation(jax.random.fold_in(rng, 2), number_of)]


def bell_draw(key, extent, scale, limit, shards=(), held_as=jnp.bfloat16):
    result = scale * jax.random.normal(key, extent, jnp.float32)
    if shards:
        result = result * shard_levels(key, extent, shards, -0.22, 0.18)
    return jnp.clip(result, -limit, limit).astype(held_as)


def setup_inputs(seed: int = 0, part: int = 0) -> dict:
    key_of = jax.random.split(jax.random.key(seed), 11)
    part_keys = jax.random.split(jax.random.fold_in(key_of[10], part), 11)
    residual = draw_residual(jax.random.fold_in(jax.random.fold_in(key_of[10], part), 71), part)
    latent = draw_latent(jax.random.fold_in(jax.random.fold_in(key_of[10], part), 71), part)
    queries = draw_queries(jax.random.fold_in(jax.random.fold_in(key_of[10], part), 71), part)
    lengths = ragged_sizes(part_keys[3], SEQS, TOKENS, TOKENS * 3 // 4, 0).astype(jnp.int32)
    value_weight = bell_draw(key_of[4], (LAT, HEADS * VHEAD), (LAT // 16) ** -0.5, 1.0, ((1, 4),))
    output_weight = bell_draw(key_of[5], (HEADS * VHEAD, D), (HEADS * VHEAD) ** -0.5, 0.0625, ((0, 4), (1, 4)))
    norm_gain = jnp.clip(1.0 + 0.18 * jax.random.normal(key_of[6], (D,), jnp.float32), 0.1, 1.9)
    gate_weight = bell_draw(key_of[7], (D, FF), D ** -0.5, 0.0625, ((0, 4), (1, 4)))
    up_weight = bell_draw(key_of[8], (D, FF), D ** -0.5, 0.0625, ((0, 4), (1, 4)))
    down_weight = bell_draw(key_of[9], (FF, D), FF ** -0.5, 0.0625, ((0, 4), (1, 4)))
    return dict(residual=residual, latent=latent, queries=queries, lengths=lengths, value_weight=value_weight, output_weight=output_weight, norm_gain=norm_gain, gate_weight=gate_weight, up_weight=up_weight, down_weight=down_weight)


score_scale = 192.0 ** (-0.5)
rope_base = 10000.0
norm_eps = 1e-06
masked_score = -1e+30

def rope_freqs(half_width):
    return rope_base ** (-jnp.arange(half_width, dtype=jnp.float32) / half_width)

def trace_info(token_index, lengths):
    trace_ends = jnp.cumsum(lengths).astype(jnp.int32)
    starts = (trace_ends - lengths).astype(jnp.int32)
    trace_ids = lax.optimization_barrier(jnp.sum((token_index[:, None] >= trace_ends[None, :]).astype(jnp.int32), axis=1)).astype(jnp.int32)
    member = trace_ids[:, None] == jnp.arange(lengths.shape[0], dtype=jnp.int32)[None, :]
    pos_shift = lax.optimization_barrier(jnp.sum(jnp.where(member, (0 - starts)[None, :], 0), axis=1)).astype(jnp.int32)
    return (trace_ids, token_index + pos_shift)

def rope_keys(latent, positions, latent_width):
    values = latent.astype(jnp.float32)
    half_width = (values.shape[0] - latent_width) // 2
    angles = rope_freqs(half_width)[:, None] * positions.astype(jnp.float32)[None, :]
    first_half = values[latent_width:latent_width + half_width]
    second_half = values[latent_width + half_width:]
    cosine = jnp.cos(angles)
    sine_value = jnp.sin(angles)
    return jnp.concatenate([values[:latent_width], first_half * cosine - second_half * sine_value, first_half * sine_value + second_half * cosine], axis=0).astype(jnp.bfloat16)

def rope_queries(queries, positions, latent_width):
    values = queries.astype(jnp.float32)
    half_width = (values.shape[2] - latent_width) // 2
    angles = positions.astype(jnp.float32)[:, None] * rope_freqs(half_width)[None, :]
    cosine = jnp.cos(angles)[:, None, :]
    sine_value = jnp.sin(angles)[:, None, :]
    first_half = values[:, :, latent_width:latent_width + half_width]
    second_half = values[:, :, latent_width + half_width:]
    return jnp.concatenate([values[:, :, :latent_width], first_half * cosine - second_half * sine_value, first_half * sine_value + second_half * cosine], axis=2).astype(jnp.bfloat16)

def add_terms(total_sum, block_pair):
    block_term = jnp.dot(block_pair[0], block_pair[1], preferred_element_type=jnp.float32).astype(jnp.bfloat16)
    return (total_sum + lax.optimization_barrier(block_term).astype(jnp.float32), None)

def reference(residual, latent, queries, lengths, value_weight, output_weight, norm_gain, gate_weight, up_weight, down_weight):
    token_count = residual.shape[0]
    token_index = jnp.arange(token_count, dtype=jnp.int32)
    trace_ids, positions = trace_info(token_index, lengths)
    keys_rot = rope_keys(latent, positions, LAT)
    rotated = rope_queries(queries.reshape(token_count, HEADS, LAT + ROPE), positions, LAT)
    allowed = (trace_ids[:, None] == trace_ids[None, :]) & (token_index[None, :] <= token_index[:, None])
    key_values = keys_rot[:LAT]

    def one_head(head_queries):
        scores = jnp.dot(head_queries, keys_rot, preferred_element_type=jnp.float32) * score_scale
        scores = jnp.where(allowed, scores, masked_score)
        row_top = lax.optimization_barrier(jnp.max(scores, axis=1, keepdims=True))
        exponent = jnp.where(allowed, jnp.exp(scores - row_top), 0.0)
        row_total = lax.optimization_barrier(jnp.sum(exponent, axis=1, keepdims=True))
        weighted = lax.dot_general(exponent.astype(jnp.bfloat16), key_values, (((1,), (1,)), ((), ())), preferred_element_type=jnp.float32)
        return (weighted / row_total).astype(jnp.bfloat16)
    mixed_latent = lax.map(one_head, jnp.transpose(rotated, (1, 0, 2)))
    head_mix = jnp.einsum('hnl,lhd->nhd', mixed_latent.astype(jnp.float32), value_weight.reshape(LAT, HEADS, VHEAD).astype(jnp.float32))
    heads_out = head_mix.astype(jnp.bfloat16).reshape(token_count, HEADS * VHEAD)
    head_blocks = heads_out.reshape(token_count, N_CTX, HGROUP).transpose(1, 0, 2)
    head_sum, _ = lax.scan(add_terms, jnp.zeros((token_count, D), jnp.float32), (head_blocks, output_weight.reshape(N_CTX, HGROUP, D)))
    attended = (residual.astype(jnp.float32) + head_sum).astype(jnp.bfloat16)
    attended_float = attended.astype(jnp.float32)
    inverse_rms = lax.rsqrt(lax.optimization_barrier(jnp.mean(attended_float * attended_float, axis=1, keepdims=True)) + norm_eps)
    scaled = (attended_float * inverse_rms * norm_gain[None, :]).astype(jnp.bfloat16)
    scaled_blocks = scaled.reshape(token_count, N_TP, DGROUP).transpose(1, 0, 2)
    zeros_units = jnp.zeros((token_count, FF), jnp.float32)
    gate_sum, _ = lax.scan(add_terms, zeros_units, (scaled_blocks, gate_weight.reshape(N_TP, DGROUP, FF)))
    up_sum, _ = lax.scan(add_terms, zeros_units, (scaled_blocks, up_weight.reshape(N_TP, DGROUP, FF)))
    hidden = (jax.nn.silu(gate_sum) * up_sum).astype(jnp.bfloat16)
    hidden_blocks = hidden.reshape(token_count, N_CTX, FGROUP).transpose(1, 0, 2)
    down_sum, _ = lax.scan(add_terms, jnp.zeros((token_count, D), jnp.float32), (hidden_blocks, down_weight.reshape(N_CTX, FGROUP, D)))
    layer_out = (attended_float + down_sum).astype(jnp.bfloat16)
    return (attended, layer_out)
```

```python
import functools

import jax
import jax.numpy as jnp
from jax import lax
from jax.experimental import pallas as pl
from jax.experimental.pallas import tpu as pltpu
from jax.sharding import PartitionSpec as P

D = 7168
LAT = 512
ROPE = 64
VHEAD = 128


score_scale = 192.0 ** (-0.5)
rope_base = 10000.0
norm_eps = 1e-06
masked_score = -1e30


def rope_freqs(half_width):
    return rope_base ** (-jnp.arange(half_width, dtype=jnp.float32) / half_width)


def trace_info(token_index, lengths):
    trace_ends = jnp.cumsum(lengths)
    starts = trace_ends - lengths
    trace_ids = jnp.sum((token_index[:, None] >= trace_ends[None, :]).astype(jnp.int32), axis=1)
    member = trace_ids[:, None] == jnp.arange(lengths.shape[0], dtype=jnp.int32)[None, :]
    pos_shift = jnp.sum(jnp.where(member, (0 - starts)[None, :], 0), axis=1)
    return (trace_ids, token_index + pos_shift)


def rope_keys(latent, positions, latent_width):
    values = latent.astype(jnp.float32)
    half_width = (values.shape[0] - latent_width) // 2
    angles = rope_freqs(half_width)[:, None] * positions.astype(jnp.float32)[None, :]
    first_half = values[latent_width : latent_width + half_width]
    second_half = values[latent_width + half_width :]
    cosine = jnp.cos(angles)
    sine_value = jnp.sin(angles)
    return jnp.concatenate(
        [
            values[:latent_width],
            first_half * cosine - second_half * sine_value,
            first_half * sine_value + second_half * cosine,
        ],
        axis=0,
    ).astype(jnp.bfloat16)


def rope_queries(queries, positions, latent_width):
    values = queries.astype(jnp.float32)
    half_width = (values.shape[2] - latent_width) // 2
    angles = positions.astype(jnp.float32)[:, None] * rope_freqs(half_width)[None, :]
    cosine = jnp.cos(angles)[:, None, :]
    sine_value = jnp.sin(angles)[:, None, :]
    first_half = values[:, :, latent_width : latent_width + half_width]
    second_half = values[:, :, latent_width + half_width :]
    return jnp.concatenate(
        [
            values[:, :, :latent_width],
            first_half * cosine - second_half * sine_value,
            first_half * sine_value + second_half * cosine,
        ],
        axis=2,
    ).astype(jnp.bfloat16)


def score_rows(state_carry, query_block, block_index, block_trace, key_piece, key_index, key_trace):
    row_top, row_total, mixed_sum = state_carry
    allowed = (key_trace[None, :] == block_trace[:, None]) & (
        key_index[None, :] <= block_index[:, None]
    )
    scores = (
        jnp.einsum("qhe,ek->hqk", query_block, key_piece, preferred_element_type=jnp.float32)
        * score_scale
    )
    scores = jnp.where(allowed[None], scores, masked_score)
    new_top = jnp.maximum(row_top, jnp.max(scores, axis=2))
    exponent = jnp.where(allowed[None], jnp.exp(scores - new_top[:, :, None]), 0.0)
    row_total = jnp.sum(exponent, axis=2)
    mixed_sum = jnp.einsum(
        "hqk,lk->hql",
        exponent.astype(jnp.bfloat16),
        key_piece[:LAT],
        preferred_element_type=jnp.float32,
    )
    return (new_top, row_total, mixed_sum)


MESH = pl.DeviceIdType.MESH
COLS = 256
VMEM_LIMIT = 60 * 1024 * 1024


def remote(src, dst, send_sem, recv_sem, ctx, tp):
    return pltpu.make_async_remote_copy(
        src_ref=src,
        dst_ref=dst,
        send_sem=send_sem,
        recv_sem=recv_sem,
        device_id={"ctx": ctx, "tp": tp},
        device_id_type=MESH,
    )


def greet(partners):
    barrier = pltpu.get_barrier_semaphore()
    for ctx, tp in partners:
        pl.semaphore_signal(
            barrier, inc=1, device_id={"ctx": ctx, "tp": tp}, device_id_type=MESH
        )
    pl.semaphore_wait(barrier, len(partners))


def greet_all(ci, ti, nc, nt):
    flat = ci * nt + ti
    partners = []
    for offset in range(1, nc * nt):
        other = lax.rem(flat + offset, nc * nt)
        partners.append((other // nt, lax.rem(other, nt)))
    greet(partners)


def line_sum(ci, ti, nc, scatter, compute, finish, part, bufs, sems):
    send_r, send_l, recv_r, recv_l = bufs
    out_r, out_l, in_r, in_l = sems
    chunks, blocks = part.shape[0], part.shape[1]

    def right(k, d):
        return remote(
            send_r.at[k, d], recv_r.at[k, d], out_r.at[k, d], in_r.at[k, d],
            lax.rem(ci + 1, nc), ti,
        )

    def left(k, d):
        return remote(
            send_l.at[k, d], recv_l.at[k, d], out_l.at[k, d], in_l.at[k, d],
            lax.rem(ci + nc - 1, nc), ti,
        )

    def forward(k, copy, send, recv, is_first, wanted):
        for d in range(blocks):

            @pl.when(wanted(d))
            def _():
                @pl.when(is_first)
                def _():
                    send[k, d] = part[k, d].astype(jnp.bfloat16)

                @pl.when(jnp.logical_not(is_first))
                def _():
                    copy(k, d).wait_recv()
                    send[k, d] = (part[k, d] + recv[k, d].astype(jnp.float32)).astype(
                        jnp.bfloat16
                    )

                copy(k, d).start()

    go_right = (lambda d: d > ci) if scatter else (lambda d: ci < nc - 1)
    go_left = (lambda d: d < ci) if scatter else (lambda d: ci > 0)

    def step(s, carry):
        @pl.when(s < chunks)
        def _():
            compute(s)

        r = s - ci

        @pl.when((ci < nc - 1) & (r >= 0) & (r < chunks))
        def _():
            forward(r, right, send_r, recv_r, ci == 0, go_right)

        l = s - (nc - 1 - ci)

        @pl.when((ci > 0) & (l >= 0) & (l < chunks))
        def _():
            forward(l, left, send_l, recv_l, ci == nc - 1, go_left)

        return carry

    lax.fori_loop(0, chunks + nc - 1, step, 0)

    def last(k, carry):
        own = ci if scatter else 0

        @pl.when(ci > 0)
        def _():
            if scatter:
                right(k, own).wait_recv()
            else:

                @pl.when(ci == nc - 1)
                def _():
                    right(k, own).wait_recv()

            part[k, own] += recv_r[k, own].astype(jnp.float32)

        @pl.when(ci < nc - 1)
        def _():
            if scatter:
                left(k, own).wait_recv()
            else:

                @pl.when(ci == 0)
                def _():
                    left(k, own).wait_recv()

            part[k, own] += recv_l[k, own].astype(jnp.float32)

        finish(k, own)
        return carry

    lax.fori_loop(0, chunks, last, 0)

    def drain(k, carry):
        for d in range(blocks):

            @pl.when(go_right(d))
            def _():
                right(k, d).wait_send()

            @pl.when(go_left(d))
            def _():
                left(k, d).wait_send()

        return carry

    lax.fori_loop(0, chunks, drain, 0)


def columns(k):
    return pl.ds(pl.multiple_of(k * COLS, COLS), COLS)


def attend_kernel(
    nc, nt, ho, w_hbm, res, out, h, w, part, b0, b1, b2, b3,
    q0, q1, q2, q3, wsem, lsem, s1, r1, s2, r2, s3, r3, s4, r4,
):
    ci, ti = lax.axis_index("ctx"), lax.axis_index("tp")
    rows = res.shape[0]
    fetch = pltpu.make_async_copy(w_hbm, w, wsem)
    fetch.start()
    greet_all(ci, ti, nc, nt)
    mate = ti + 1 - 2 * lax.rem(ti, 2)
    across = lax.rem(ti + 2, nt)
    mine = ci == ti

    def first(q, c):
        return remote(ho.at[q], h.at[c, q], s1.at[q], r1.at[c], ti, q)

    for q in range(nt):
        to_self = mine & (ti == q)

        @pl.when(to_self)
        def _():
            pltpu.make_async_copy(ho.at[q], h.at[ci, q], lsem).start()

        @pl.when(jnp.logical_not(to_self))
        def _():
            first(q, ci).start()

    def to_mate(c):
        return remote(h.at[c, ti], h.at[c, ti], s2.at[c], r2.at[c], ci, mate)

    def to_across(c):
        return remote(h.at[c, ti], h.at[c, ti], s3.at[c], r3.at[c], ci, across)

    def relay(c):
        return remote(h.at[c, across], h.at[c, across], s4.at[c], r4.at[c], ci, mate)

    for c in range(nc):
        from_self = mine & (ci == c)

        @pl.when(from_self)
        def _():
            pltpu.make_async_copy(ho.at[ti], h.at[c, ti], lsem).wait()

        @pl.when(jnp.logical_not(from_self))
        def _():
            remote(ho.at[ti], h.at[c, ti], s1.at[ti], r1.at[c], ci, mate).wait_recv()

        to_across(c).start()
        to_mate(c).start()
    for c in range(nc):
        remote(h.at[c, across], h.at[c, across], s3.at[c], r3.at[c], ci, across).wait_recv()
        relay(c).start()
    far = lax.rem(mate + 2, nt)
    for c in range(nc):
        remote(h.at[c, mate], h.at[c, mate], s2.at[c], r2.at[c], ci, mate).wait_recv()
        remote(h.at[c, far], h.at[c, far], s4.at[c], r4.at[c], ci, mate).wait_recv()
    fetch.wait()

    def compute(k):
        part[k, 0] = jnp.dot(
            h[...].reshape(nc * rows, h.shape[3]),
            w[:, columns(k)],
            preferred_element_type=jnp.float32,
        )
        own = pl.ds(pl.multiple_of(ci * rows, rows), rows)
        part[k, 0, own, :] += res[:, columns(k)].astype(jnp.float32)

    def finish(k, own):
        out[:, columns(k)] = part[k, 0].astype(jnp.bfloat16)

    line_sum(ci, ti, nc, False, compute, finish, part, (b0, b1, b2, b3), (q0, q1, q2, q3))
    for q in range(nt):

        @pl.when(jnp.logical_not(mine & (ti == q)))
        def _():
            first(q, ci).wait_send()

    for c in range(nc):
        to_mate(c).wait_send()
        to_across(c).wait_send()
        relay(c).wait_send()


def attend_call(nc, nt, heads_out, output_weight, residual):
    rows, width = residual.shape
    depth = output_weight.shape[0]
    chunks = width // COLS
    buf = pltpu.VMEM((chunks, 1, nc * rows, COLS), jnp.bfloat16)
    sem = pltpu.SemaphoreType.DMA((chunks, 1))
    return pl.pallas_call(
        functools.partial(attend_kernel, nc, nt),
        out_shape=jax.ShapeDtypeStruct((nc * rows, width), jnp.bfloat16),
        in_specs=[
            pl.BlockSpec(memory_space=pltpu.VMEM),
            pl.BlockSpec(memory_space=pl.ANY),
            pl.BlockSpec(memory_space=pltpu.VMEM),
        ],
        out_specs=pl.BlockSpec(memory_space=pltpu.VMEM),
        scratch_shapes=[
            pltpu.VMEM((nc, nt, rows // nt, depth), jnp.bfloat16),
            pltpu.VMEM((depth, width), jnp.bfloat16),
            pltpu.VMEM((chunks, 1, nc * rows, COLS), jnp.float32),
        ]
        + [buf] * 4
        + [sem] * 4
        + [pltpu.SemaphoreType.DMA, pltpu.SemaphoreType.DMA]
        + [pltpu.SemaphoreType.DMA((nt,)), pltpu.SemaphoreType.DMA((nc,))]
        + [pltpu.SemaphoreType.DMA((nc,))] * 6,
        compiler_params=pltpu.CompilerParams(
            collective_id=0, has_side_effects=True, vmem_limit_bytes=VMEM_LIMIT
        ),
    )(heads_out.reshape(nt, rows // nt, depth), output_weight, residual)


def hidden_kernel(
    nt, x, squares, gate_hbm, up_hbm, out, gate, up, g_all, kept, sa, ra, sb, rb, hb, sq,
    gsem, usem, sqs, sqr, sas, sar, sbs, sbr, hxs, hxr, hcs, hcr, hfs, hfr,
):
    ci, ti = lax.axis_index("ctx"), lax.axis_index("tp")
    chunks = gsem.shape[0]
    rows = squares.shape[1]

    def get(k, hbm, held, sem):
        return pltpu.make_async_copy(hbm.at[:, columns(k)], held.at[:, columns(k)], sem.at[k])

    for k in range(chunks):
        get(k, gate_hbm, gate, gsem).start()
        get(k, up_hbm, up, usem).start()
    greet([(ci, lax.rem(ti + o, nt)) for o in range(1, nt)])
    mate = ti + 1 - 2 * lax.rem(ti, 2)
    across = lax.rem(ti + 2, nt)
    far = lax.rem(mate + 2, nt)
    core = lax.rem(ti, 2)
    side = ti // 2

    def send_squares(o):
        other = lax.rem(ti + o, nt)
        return remote(
            squares.at[other], sq.at[o - 1], sqs.at[o - 1], sqr.at[o - 1], ci, other
        )

    for o in range(1, nt):
        send_squares(o).start()

    def to_mate(k):
        return remote(sa.at[k], ra.at[k], sas.at[k], sar.at[k], ci, mate)

    def to_across(k):
        return remote(sb.at[k], rb.at[k], sbs.at[k], sbr.at[k], ci, across)

    def hid(k, owner, send, recv, target):
        return remote(hb.at[k, owner], hb.at[k, owner], send.at[k], recv.at[k], ci, target)

    total = squares[ti]
    for o in range(1, nt):
        send_squares(o).wait_recv()
        total = total + sq[o - 1]
    sq[0] = lax.rsqrt(total / D + norm_eps)

    def step(s, carry):
        @pl.when(s < chunks)
        def _():
            get(s, gate_hbm, gate, gsem).wait()
            get(s, up_hbm, up, usem).wait()
            for place, held in ((0, gate), (1, up)):
                g_all[:, :, place * COLS : (place + 1) * COLS] = jnp.dot(
                    x[...], held[:, columns(s)], preferred_element_type=jnp.float32
                ).reshape(nt, rows, COLS)
            for i in range(nt // 2):
                sa[s, i] = g_all[2 * i + 1 - core].astype(jnp.bfloat16)
                kept[s, i] = g_all[2 * i + core]
            to_mate(s).start()

        a = s - 1

        @pl.when((a >= 0) & (a < chunks))
        def _():
            to_mate(a).wait_recv()
            sb[a] = (kept[a, 1 - side] + ra[a, 1 - side].astype(jnp.float32)).astype(
                jnp.bfloat16
            )
            to_across(a).start()
            kept[a, side] += ra[a, side].astype(jnp.float32)

        b = s - 3

        @pl.when((b >= 0) & (b < chunks))
        def _():
            to_across(b).wait_recv()
            inverse = sq[0][:, :1]
            summed = (kept[b, side] + rb[b].astype(jnp.float32)) * inverse
            hb[b, ti] = (jax.nn.silu(summed[:, :COLS]) * summed[:, COLS:]).astype(jnp.bfloat16)
            hid(b, ti, hxs, hxr, across).start()
            hid(b, ti, hcs, hcr, mate).start()

        c = s - 5

        @pl.when((c >= 0) & (c < chunks))
        def _():
            hid(c, across, hxs, hxr, across).wait_recv()
            hid(c, across, hfs, hfr, mate).start()

        return carry

    lax.fori_loop(0, chunks + 5, step, 0)

    def last(k, carry):
        hid(k, mate, hcs, hcr, mate).wait_recv()
        hid(k, far, hfs, hfr, mate).wait_recv()
        out[:, columns(k)] = hb[k].reshape(nt * rows, COLS)
        to_mate(k).wait_send()
        to_across(k).wait_send()
        hid(k, ti, hxs, hxr, across).wait_send()
        hid(k, ti, hcs, hcr, mate).wait_send()
        hid(k, across, hfs, hfr, mate).wait_send()
        return carry

    lax.fori_loop(0, chunks, last, 0)
    for o in range(1, nt):
        send_squares(o).wait_send()


def hidden_call(nt, x, squares, gate_weight, up_weight):
    tokens, width = x.shape
    units = gate_weight.shape[1]
    rows = tokens // nt
    chunks = units // COLS
    sem = pltpu.SemaphoreType.DMA((chunks,))
    return pl.pallas_call(
        functools.partial(hidden_kernel, nt),
        out_shape=jax.ShapeDtypeStruct((tokens, units), jnp.bfloat16),
        in_specs=[pl.BlockSpec(memory_space=pltpu.VMEM)] * 2
        + [pl.BlockSpec(memory_space=pl.ANY)] * 2,
        out_specs=pl.BlockSpec(memory_space=pltpu.VMEM),
        scratch_shapes=[
            pltpu.VMEM((width, units), jnp.bfloat16),
            pltpu.VMEM((width, units), jnp.bfloat16),
            pltpu.VMEM((nt, rows, 2 * COLS), jnp.float32),
            pltpu.VMEM((chunks, nt // 2, rows, 2 * COLS), jnp.float32),
            pltpu.VMEM((chunks, nt // 2, rows, 2 * COLS), jnp.bfloat16),
            pltpu.VMEM((chunks, nt // 2, rows, 2 * COLS), jnp.bfloat16),
            pltpu.VMEM((chunks, rows, 2 * COLS), jnp.bfloat16),
            pltpu.VMEM((chunks, rows, 2 * COLS), jnp.bfloat16),
            pltpu.VMEM((chunks, nt, rows, COLS), jnp.bfloat16),
            pltpu.VMEM((nt - 1, rows, 128), jnp.float32),
            sem,
            sem,
            pltpu.SemaphoreType.DMA((nt - 1,)),
            pltpu.SemaphoreType.DMA((nt - 1,)),
        ]
        + [sem] * 10,
        compiler_params=pltpu.CompilerParams(
            collective_id=1, has_side_effects=True, vmem_limit_bytes=VMEM_LIMIT
        ),
    )(x, squares, gate_weight, up_weight)


def down_kernel(
    nc, hidden, w_hbm, base, out, w, part, b0, b1, b2, b3, q0, q1, q2, q3, wsem
):
    ci, ti = lax.axis_index("ctx"), lax.axis_index("tp")
    rows = base.shape[0]
    chunks = part.shape[0]

    def get(k):
        return pltpu.make_async_copy(w_hbm.at[:, columns(k)], w.at[:, columns(k)], wsem.at[k])

    for k in range(chunks):
        get(k).start()
    greet([(lax.rem(ci + o, nc), ti) for o in range(1, nc)])

    def compute(k):
        get(k).wait()
        part[k] = jnp.dot(
            hidden[...], w[:, columns(k)], preferred_element_type=jnp.float32
        ).reshape(nc, rows, COLS)

    def finish(k, own):
        out[:, columns(k)] = (part[k, own] + base[:, columns(k)].astype(jnp.float32)).astype(
            jnp.bfloat16
        )

    line_sum(ci, ti, nc, True, compute, finish, part, (b0, b1, b2, b3), (q0, q1, q2, q3))


def down_call(nc, hidden, down_weight, attended):
    rows, width = attended.shape
    depth = down_weight.shape[0]
    chunks = width // COLS
    return pl.pallas_call(
        functools.partial(down_kernel, nc),
        out_shape=jax.ShapeDtypeStruct((rows, width), jnp.bfloat16),
        in_specs=[
            pl.BlockSpec(memory_space=pltpu.VMEM),
            pl.BlockSpec(memory_space=pl.ANY),
            pl.BlockSpec(memory_space=pltpu.VMEM),
        ],
        out_specs=pl.BlockSpec(memory_space=pltpu.VMEM),
        scratch_shapes=[
            pltpu.VMEM((depth, width), jnp.bfloat16),
            pltpu.VMEM((chunks, nc, rows, COLS), jnp.float32),
        ]
        + [pltpu.VMEM((chunks, nc, rows, COLS), jnp.bfloat16)] * 4
        + [pltpu.SemaphoreType.DMA((chunks, nc))] * 4
        + [pltpu.SemaphoreType.DMA((chunks,))],
        compiler_params=pltpu.CompilerParams(
            collective_id=2, has_side_effects=True, vmem_limit_bytes=VMEM_LIMIT
        ),
    )(hidden, down_weight, attended)


def kernels_fit(nc, nt, rows, width, depth, units):
    tokens = nc * rows
    attend = 2 * depth * width + 2 * tokens * depth + 16 * tokens * width
    middle = 4 * width * units + 20 * tokens * units + 2 * tokens * width
    down = 2 * units * width + 2 * tokens * units + 14 * tokens * width
    return (
        nt == 4
        and nc == nt
        and rows % (16 * nt) == 0
        and width % COLS == 0
        and units % COLS == 0
        and max(attend, middle, down) < VMEM_LIMIT - 2 * 1024 * 1024
    )


def on_device(
    residual,
    latent,
    queries,
    lengths,
    value_weight,
    output_weight,
    norm_gain,
    gate_weight,
    up_weight,
    down_weight,
):
    row_count = residual.shape[0]
    ctx_place = lax.axis_index("ctx")
    local_heads = value_weight.shape[1] // VHEAD
    own_index = ctx_place * row_count + jnp.arange(row_count, dtype=jnp.int32)
    own_trace, own_position = trace_info(own_index, lengths)
    rotated_keys = rope_keys(latent, own_position, LAT)
    rotated_queries = rope_queries(
        queries.reshape(row_count, local_heads, LAT + ROPE), own_position, LAT
    )
    last_query = ctx_place * row_count + row_count - 1
    start_state = (
        jnp.full((local_heads, row_count), masked_score, jnp.float32),
        jnp.zeros((local_heads, row_count), jnp.float32),
        jnp.zeros((local_heads, row_count, LAT), jnp.float32),
    )
    key_piece = lax.all_gather(rotated_keys, "ctx", axis=1, tiled=True)
    key_index = jnp.arange(key_piece.shape[1], dtype=jnp.int32)
    key_trace, _ = trace_info(key_index, lengths)
    folded = lax.cond(
        jnp.int32(0) <= last_query,
        lambda held: score_rows(
            held, rotated_queries, own_index, own_trace, key_piece, key_index, key_trace
        ),
        lambda held: held,
        start_state,
    )
    row_top, row_total, mixed_sum = folded
    mixed_latent = (mixed_sum / row_total[:, :, None]).astype(jnp.bfloat16)
    heads_out = (
        jnp.einsum(
            "hql,lhd->qhd",
            mixed_latent,
            value_weight.reshape(LAT, local_heads, VHEAD),
            preferred_element_type=jnp.float32,
        )
        .astype(jnp.bfloat16)
        .reshape(row_count, local_heads * VHEAD)
    )
    nc, nt = lax.axis_size("ctx"), lax.axis_size("tp")
    if kernels_fit(
        nc, nt, row_count, residual.shape[1], output_weight.shape[0], gate_weight.shape[1]
    ):
        attended_all = attend_call(nc, nt, heads_out, output_weight, residual)
        attended = lax.dynamic_slice_in_dim(attended_all, ctx_place * row_count, row_count, 0)
        wide = attended_all.astype(jnp.float32)
        squares = jnp.sum(wide * wide, axis=1)
        squares = jnp.broadcast_to(squares[:, None], (nc * row_count, 128)).reshape(
            nt, nc * row_count // nt, 128
        )
        gained = (wide * norm_gain[None, :]).astype(jnp.bfloat16)
        hidden = hidden_call(nt, gained, squares, gate_weight, up_weight)
        return (attended, down_call(nc, hidden, down_weight, attended))
    all_heads = lax.all_gather(heads_out, "tp", axis=1, tiled=True)
    head_block = lax.all_to_all(all_heads, "ctx", split_axis=1, concat_axis=0, tiled=True)
    head_sum = lax.psum_scatter(
        jnp.dot(head_block, output_weight, preferred_element_type=jnp.float32).astype(jnp.bfloat16),
        "ctx",
        scatter_dimension=0,
        tiled=True,
    ).astype(jnp.float32)
    attended = (residual.astype(jnp.float32) + head_sum).astype(jnp.bfloat16)
    attended_float = attended.astype(jnp.float32)
    squares = lax.psum(jnp.sum(attended_float * attended_float, axis=1), "tp")
    inverse_rms = lax.rsqrt(squares / D + norm_eps)
    scaled = (attended_float * inverse_rms[:, None] * norm_gain[None, :]).astype(jnp.bfloat16)
    scaled_all = lax.all_gather(scaled, "ctx", axis=0, tiled=True)
    unit_count = gate_weight.shape[1]
    gate_up = jnp.concatenate([gate_weight, up_weight], axis=1)
    summed = lax.psum_scatter(
        jnp.dot(scaled_all, gate_up, preferred_element_type=jnp.float32).astype(jnp.bfloat16),
        "tp",
        scatter_dimension=0,
        tiled=True,
    ).astype(jnp.float32)
    hidden_share = (jax.nn.silu(summed[:, :unit_count]) * summed[:, unit_count:]).astype(
        jnp.bfloat16
    )
    hidden_all = lax.all_gather(hidden_share, "tp", axis=0, tiled=True)
    down_sum = lax.psum_scatter(
        jnp.dot(hidden_all, down_weight, preferred_element_type=jnp.float32).astype(jnp.bfloat16),
        "ctx",
        scatter_dimension=0,
        tiled=True,
    ).astype(jnp.float32)
    layer_out = (attended_float + down_sum).astype(jnp.bfloat16)
    return (attended, layer_out)


def solution(mesh):
    in_specs = (
        P(("grp", "ctx"), "tp"),
        P(None, ("grp", "ctx")),
        P(("grp", "ctx"), "tp"),
        P("grp"),
        P(None, "tp"),
        P("ctx", "tp"),
        P("tp"),
        P("tp", "ctx"),
        P("tp", "ctx"),
        P("ctx", "tp"),
    )
    out_specs = (P(("grp", "ctx"), "tp"), P(("grp", "ctx"), "tp"))
    return jax.shard_map(
        on_device, mesh=mesh, in_specs=in_specs, out_specs=out_specs, check_vma=False
    )
```

```python
import functools

import jax
import jax.numpy as jnp
from jax import lax
from jax.experimental import pallas as pl
from jax.experimental.pallas import tpu as pltpu
from jax.sharding import PartitionSpec as P

D = 7168
LAT = 512
ROPE = 64
VHEAD = 128


score_scale = 192.0 ** (-0.5)
rope_base = 10000.0
norm_eps = 1e-06
masked_score = -1e30


def rope_freqs(half_width):
    return rope_base ** (-jnp.arange(half_width, dtype=jnp.float32) / half_width)


def trace_info(token_index, lengths):
    trace_ends = jnp.cumsum(lengths)
    starts = trace_ends - lengths
    trace_ids = jnp.sum((token_index[:, None] >= trace_ends[None, :]).astype(jnp.int32), axis=1)
    member = trace_ids[:, None] == jnp.arange(lengths.shape[0], dtype=jnp.int32)[None, :]
    pos_shift = jnp.sum(jnp.where(member, (0 - starts)[None, :], 0), axis=1)
    return (trace_ids, token_index + pos_shift)


def rope_keys(latent, positions, latent_width):
    values = latent.astype(jnp.float32)
    half_width = (values.shape[0] - latent_width) // 2
    angles = rope_freqs(half_width)[:, None] * positions.astype(jnp.float32)[None, :]
    first_half = values[latent_width : latent_width + half_width]
    second_half = values[latent_width + half_width :]
    cosine = jnp.cos(angles)
    sine_value = jnp.sin(angles)
    return jnp.concatenate(
        [
            values[:latent_width],
            first_half * cosine - second_half * sine_value,
            first_half * sine_value + second_half * cosine,
        ],
        axis=0,
    ).astype(jnp.bfloat16)


def rope_queries(queries, positions, latent_width):
    values = queries.astype(jnp.float32)
    half_width = (values.shape[2] - latent_width) // 2
    angles = positions.astype(jnp.float32)[:, None] * rope_freqs(half_width)[None, :]
    cosine = jnp.cos(angles)[:, None, :]
    sine_value = jnp.sin(angles)[:, None, :]
    first_half = values[:, :, latent_width : latent_width + half_width]
    second_half = values[:, :, latent_width + half_width :]
    return jnp.concatenate(
        [
            values[:, :, :latent_width],
            first_half * cosine - second_half * sine_value,
            first_half * sine_value + second_half * cosine,
        ],
        axis=2,
    ).astype(jnp.bfloat16)


def score_rows(state_carry, query_block, block_index, block_trace, key_piece, key_index, key_trace):
    row_top, row_total, mixed_sum = state_carry
    allowed = (key_trace[None, :] == block_trace[:, None]) & (
        key_index[None, :] <= block_index[:, None]
    )
    scores = (
        jnp.einsum("qhe,ek->hqk", query_block, key_piece, preferred_element_type=jnp.float32)
        * score_scale
    )
    scores = jnp.where(allowed[None], scores, masked_score)
    new_top = jnp.maximum(row_top, jnp.max(scores, axis=2))
    exponent = jnp.where(allowed[None], jnp.exp(scores - new_top[:, :, None]), 0.0)
    row_total = jnp.sum(exponent, axis=2)
    mixed_sum = jnp.einsum(
        "hqk,lk->hql",
        exponent.astype(jnp.bfloat16),
        key_piece[:LAT],
        preferred_element_type=jnp.float32,
    )
    return (new_top, row_total, mixed_sum)


MESH = pl.DeviceIdType.MESH
COLS = 256
LANES = 128
VMEM_LIMIT = 60 * 1024 * 1024


def remote(src, dst, send_sem, recv_sem, ctx, tp):
    return pltpu.make_async_remote_copy(
        src_ref=src,
        dst_ref=dst,
        send_sem=send_sem,
        recv_sem=recv_sem,
        device_id={"ctx": ctx, "tp": tp},
        device_id_type=MESH,
    )


def greet(partners):
    barrier = pltpu.get_barrier_semaphore()
    for ctx, tp in partners:
        pl.semaphore_signal(
            barrier, inc=1, device_id={"ctx": ctx, "tp": tp}, device_id_type=MESH
        )
    pl.semaphore_wait(barrier, len(partners))


def greet_all(ci, ti, nc, nt):
    flat = ci * nt + ti
    partners = []
    for offset in range(1, nc * nt):
        other = lax.rem(flat + offset, nc * nt)
        partners.append((other // nt, lax.rem(other, nt)))
    greet(partners)


def line_sum(ci, ti, nc, scatter, compute, finish, part, bufs, sems):
    send_r, send_l, recv_r, recv_l = bufs
    out_r, out_l, in_r, in_l = sems
    chunks, blocks = part.shape[0], part.shape[1]

    def right(k, d):
        return remote(
            send_r.at[k, d], recv_r.at[k, d], out_r.at[k, d], in_r.at[k, d],
            lax.rem(ci + 1, nc), ti,
        )

    def left(k, d):
        return remote(
            send_l.at[k, d], recv_l.at[k, d], out_l.at[k, d], in_l.at[k, d],
            lax.rem(ci + nc - 1, nc), ti,
        )

    def forward(k, copy, send, recv, is_first, wanted):
        for d in range(blocks):

            @pl.when(wanted(d))
            def _():
                @pl.when(is_first)
                def _():
                    send[k, d] = part[k, d].astype(jnp.bfloat16)

                @pl.when(jnp.logical_not(is_first))
                def _():
                    copy(k, d).wait_recv()
                    send[k, d] = (part[k, d] + recv[k, d].astype(jnp.float32)).astype(
                        jnp.bfloat16
                    )

                copy(k, d).start()

    go_right = (lambda d: d > ci) if scatter else (lambda d: ci < nc - 1)
    go_left = (lambda d: d < ci) if scatter else (lambda d: ci > 0)

    def step(s, carry):
        @pl.when(s < chunks)
        def _():
            compute(s)

        r = s - ci

        @pl.when((ci < nc - 1) & (r >= 0) & (r < chunks))
        def _():
            forward(r, right, send_r, recv_r, ci == 0, go_right)

        l = s - (nc - 1 - ci)

        @pl.when((ci > 0) & (l >= 0) & (l < chunks))
        def _():
            forward(l, left, send_l, recv_l, ci == nc - 1, go_left)

        return carry

    lax.fori_loop(0, chunks + nc - 1, step, 0)

    def last(k, carry):
        own = ci if scatter else 0

        @pl.when(ci > 0)
        def _():
            if scatter:
                right(k, own).wait_recv()
            else:

                @pl.when(ci == nc - 1)
                def _():
                    right(k, own).wait_recv()

            part[k, own] += recv_r[k, own].astype(jnp.float32)

        @pl.when(ci < nc - 1)
        def _():
            if scatter:
                left(k, own).wait_recv()
            else:

                @pl.when(ci == 0)
                def _():
                    left(k, own).wait_recv()

            part[k, own] += recv_l[k, own].astype(jnp.float32)

        finish(k, own)
        return carry

    lax.fori_loop(0, chunks, last, 0)

    def drain(k, carry):
        for d in range(blocks):

            @pl.when(go_right(d))
            def _():
                right(k, d).wait_send()

            @pl.when(go_left(d))
            def _():
                left(k, d).wait_send()

        return carry

    lax.fori_loop(0, chunks, drain, 0)


def columns(k):
    return pl.ds(pl.multiple_of(k * COLS, COLS), COLS)


def keys_kernel(nc, nt, keys, out, held, s1, r1, s2, r2):
    ci, ti = lax.axis_index("ctx"), lax.axis_index("tp")
    height, width = keys.shape
    half = height // 2
    core = lax.rem(ti, 2)
    mate = ti + 1 - 2 * core
    greet([(lax.rem(ci + o, nc), ti) for o in range(1, nc)] + [(ci, mate)])

    def place(c):
        return pl.ds(pl.multiple_of(c * width, width), width)

    def share(which):
        return pl.ds(pl.multiple_of(which * half, half), half)

    def across(o):
        return remote(
            keys.at[share(core), :], held.at[share(core), place(ci)], s1.at[o - 1],
            r1.at[o - 1], lax.rem(ci + o, nc), ti,
        )

    def to_mate(o, which):
        spot = held.at[share(which), place(lax.rem(ci + nc - o, nc))]
        return remote(spot, spot, s2.at[o - 1], r2.at[o - 1], ci, mate)

    def arrived(o):
        spot = held.at[share(core), place(lax.rem(ci + nc - o, nc))]
        return remote(spot, spot, s1.at[o - 1], r1.at[o - 1], ci, mate)

    for o in range(1, nc):
        across(o).start()
    held[:, place(ci)] = keys[...]
    for o in range(1, nc):
        arrived(o).wait_recv()
        to_mate(o, core).start()
    for o in range(1, nc):
        to_mate(o, 1 - core).wait_recv()
    for o in range(1, nc):
        across(o).wait_send()
        to_mate(o, core).wait_send()
    out[...] = held[...]


def keys_call(nc, nt, keys):
    height, width = keys.shape
    sem = pltpu.SemaphoreType.DMA((nc - 1,))
    return pl.pallas_call(
        functools.partial(keys_kernel, nc, nt),
        out_shape=jax.ShapeDtypeStruct((height, nc * width), jnp.bfloat16),
        in_specs=[pl.BlockSpec(memory_space=pltpu.VMEM)],
        out_specs=pl.BlockSpec(memory_space=pltpu.VMEM),
        scratch_shapes=[pltpu.VMEM((height, nc * width), jnp.bfloat16)] + [sem] * 4,
        compiler_params=pltpu.CompilerParams(collective_id=3, has_side_effects=True),
    )(keys)


def attend_kernel(
    nc, nt, ho, w_hbm, res, gain, att, x, squares, h, w, part, b0, b1, b2, b3,
    q0, q1, q2, q3, wsem, lsem, s1, r1, s2, r2, s3, r3, s4, r4,
):
    ci, ti = lax.axis_index("ctx"), lax.axis_index("tp")
    rows = res.shape[0]
    fetch = pltpu.make_async_copy(w_hbm, w, wsem)
    fetch.start()
    greet_all(ci, ti, nc, nt)
    mate = ti + 1 - 2 * lax.rem(ti, 2)
    across = lax.rem(ti + 2, nt)
    mine = ci == ti

    def first(q, c):
        return remote(ho.at[q], h.at[c, q], s1.at[q], r1.at[c], ti, q)

    for q in range(nt):
        to_self = mine & (ti == q)

        @pl.when(to_self)
        def _():
            pltpu.make_async_copy(ho.at[q], h.at[ci, q], lsem).start()

        @pl.when(jnp.logical_not(to_self))
        def _():
            first(q, ci).start()

    def to_mate(c):
        return remote(h.at[c, ti], h.at[c, ti], s2.at[c], r2.at[c], ci, mate)

    def to_across(c):
        return remote(h.at[c, ti], h.at[c, ti], s3.at[c], r3.at[c], ci, across)

    def relay(c):
        return remote(h.at[c, across], h.at[c, across], s4.at[c], r4.at[c], ci, mate)

    for c in range(nc):
        from_self = mine & (ci == c)

        @pl.when(from_self)
        def _():
            pltpu.make_async_copy(ho.at[ti], h.at[c, ti], lsem).wait()

        @pl.when(jnp.logical_not(from_self))
        def _():
            remote(ho.at[ti], h.at[c, ti], s1.at[ti], r1.at[c], ci, mate).wait_recv()

        to_across(c).start()
        to_mate(c).start()
    for c in range(nc):
        remote(h.at[c, across], h.at[c, across], s3.at[c], r3.at[c], ci, across).wait_recv()
        relay(c).start()
    far = lax.rem(mate + 2, nt)
    for c in range(nc):
        remote(h.at[c, mate], h.at[c, mate], s2.at[c], r2.at[c], ci, mate).wait_recv()
        remote(h.at[c, far], h.at[c, far], s4.at[c], r4.at[c], ci, mate).wait_recv()
    fetch.wait()

    def compute(k):
        part[k, 0] = jnp.dot(
            h[...].reshape(nc * rows, h.shape[3]),
            w[:, columns(k)],
            preferred_element_type=jnp.float32,
        )
        own = pl.ds(pl.multiple_of(ci * rows, rows), rows)
        part[k, 0, own, :] += res[:, columns(k)].astype(jnp.float32)

    squares[...] = jnp.zeros_like(squares)

    def finish(k, own):
        total = part[k, 0].astype(jnp.bfloat16).astype(jnp.float32)
        x[:, columns(k)] = (total * gain[:, columns(k)]).astype(jnp.bfloat16)
        power = total * total
        squares[...] += sum(power[:, i : i + LANES] for i in range(0, COLS, LANES))
        place = pl.ds(pl.multiple_of(ci * rows, rows), rows)
        att[:, columns(k)] = part[k, 0, place, :].astype(jnp.bfloat16)

    line_sum(ci, ti, nc, False, compute, finish, part, (b0, b1, b2, b3), (q0, q1, q2, q3))
    for q in range(nt):

        @pl.when(jnp.logical_not(mine & (ti == q)))
        def _():
            first(q, ci).wait_send()

    for c in range(nc):
        to_mate(c).wait_send()
        to_across(c).wait_send()
        relay(c).wait_send()


def attend_call(nc, nt, heads_out, output_weight, residual, gain):
    rows, width = residual.shape
    depth = output_weight.shape[0]
    chunks = width // COLS
    buf = pltpu.VMEM((chunks, 1, nc * rows, COLS), jnp.bfloat16)
    sem = pltpu.SemaphoreType.DMA((chunks, 1))
    return pl.pallas_call(
        functools.partial(attend_kernel, nc, nt),
        out_shape=(
            jax.ShapeDtypeStruct((rows, width), jnp.bfloat16),
            jax.ShapeDtypeStruct((nc * rows, width), jnp.bfloat16),
            jax.ShapeDtypeStruct((nc * rows, LANES), jnp.float32),
        ),
        in_specs=[
            pl.BlockSpec(memory_space=pltpu.VMEM),
            pl.BlockSpec(memory_space=pl.ANY),
            pl.BlockSpec(memory_space=pltpu.VMEM),
            pl.BlockSpec(memory_space=pltpu.VMEM),
        ],
        out_specs=[pl.BlockSpec(memory_space=pltpu.VMEM)] * 3,
        scratch_shapes=[
            pltpu.VMEM((nc, nt, rows // nt, depth), jnp.bfloat16),
            pltpu.VMEM((depth, width), jnp.bfloat16),
            pltpu.VMEM((chunks, 1, nc * rows, COLS), jnp.float32),
        ]
        + [buf] * 4
        + [sem] * 4
        + [pltpu.SemaphoreType.DMA, pltpu.SemaphoreType.DMA]
        + [pltpu.SemaphoreType.DMA((nt,)), pltpu.SemaphoreType.DMA((nc,))]
        + [pltpu.SemaphoreType.DMA((nc,))] * 6,
        compiler_params=pltpu.CompilerParams(
            collective_id=0, has_side_effects=True, vmem_limit_bytes=VMEM_LIMIT
        ),
    )(heads_out.reshape(nt, rows // nt, depth), output_weight, residual, gain[None, :])


def hidden_kernel(
    nt, x, squares, gate_hbm, up_hbm, out, gate, up, g_all, kept, sa, ra, sb, rb, hb, sq,
    gsem, usem, sqs, sqr, sas, sar, sbs, sbr, hxs, hxr, hcs, hcr, hfs, hfr,
):
    ci, ti = lax.axis_index("ctx"), lax.axis_index("tp")
    chunks = gsem.shape[0]
    rows = squares.shape[1]

    def get(k, hbm, held, sem):
        return pltpu.make_async_copy(hbm.at[:, columns(k)], held.at[:, columns(k)], sem.at[k])

    for k in range(chunks):
        get(k, gate_hbm, gate, gsem).start()
        get(k, up_hbm, up, usem).start()
    greet([(ci, lax.rem(ti + o, nt)) for o in range(1, nt)])
    mate = ti + 1 - 2 * lax.rem(ti, 2)
    across = lax.rem(ti + 2, nt)
    far = lax.rem(mate + 2, nt)
    core = lax.rem(ti, 2)
    side = ti // 2

    def send_squares(o):
        other = lax.rem(ti + o, nt)
        return remote(
            squares.at[other], sq.at[o - 1], sqs.at[o - 1], sqr.at[o - 1], ci, other
        )

    for o in range(1, nt):
        send_squares(o).start()

    def to_mate(k):
        return remote(sa.at[k], ra.at[k], sas.at[k], sar.at[k], ci, mate)

    def to_across(k):
        return remote(sb.at[k], rb.at[k], sbs.at[k], sbr.at[k], ci, across)

    def hid(k, owner, send, recv, target):
        return remote(hb.at[k, owner], hb.at[k, owner], send.at[k], recv.at[k], ci, target)

    total = squares[ti]
    for o in range(1, nt):
        send_squares(o).wait_recv()
        total = total + sq[o - 1]
    mean = jnp.sum(total, axis=1, keepdims=True) / D
    sq[0] = jnp.broadcast_to(lax.rsqrt(mean + norm_eps), total.shape)

    def step(s, carry):
        @pl.when(s < chunks)
        def _():
            get(s, gate_hbm, gate, gsem).wait()
            get(s, up_hbm, up, usem).wait()
            for place, held in ((0, gate), (1, up)):
                g_all[:, :, place * COLS : (place + 1) * COLS] = jnp.dot(
                    x[...], held[:, columns(s)], preferred_element_type=jnp.float32
                ).reshape(nt, rows, COLS)
            for i in range(nt // 2):
                sa[s, i] = g_all[2 * i + 1 - core].astype(jnp.bfloat16)
                kept[s, i] = g_all[2 * i + core]
            to_mate(s).start()

        a = s - 1

        @pl.when((a >= 0) & (a < chunks))
        def _():
            to_mate(a).wait_recv()
            sb[a] = (kept[a, 1 - side] + ra[a, 1 - side].astype(jnp.float32)).astype(
                jnp.bfloat16
            )
            to_across(a).start()
            kept[a, side] += ra[a, side].astype(jnp.float32)

        b = s - 3

        @pl.when((b >= 0) & (b < chunks))
        def _():
            to_across(b).wait_recv()
            inverse = sq[0][:, :1]
            summed = (kept[b, side] + rb[b].astype(jnp.float32)) * inverse
            hb[b, ti] = (jax.nn.silu(summed[:, :COLS]) * summed[:, COLS:]).astype(jnp.bfloat16)
            hid(b, ti, hxs, hxr, across).start()
            hid(b, ti, hcs, hcr, mate).start()

        c = s - 5

        @pl.when((c >= 0) & (c < chunks))
        def _():
            hid(c, across, hxs, hxr, across).wait_recv()
            hid(c, across, hfs, hfr, mate).start()

        return carry

    lax.fori_loop(0, chunks + 5, step, 0)

    def last(k, carry):
        hid(k, mate, hcs, hcr, mate).wait_recv()
        hid(k, far, hfs, hfr, mate).wait_recv()
        out[:, columns(k)] = hb[k].reshape(nt * rows, COLS)
        to_mate(k).wait_send()
        to_across(k).wait_send()
        hid(k, ti, hxs, hxr, across).wait_send()
        hid(k, ti, hcs, hcr, mate).wait_send()
        hid(k, across, hfs, hfr, mate).wait_send()
        return carry

    lax.fori_loop(0, chunks, last, 0)
    for o in range(1, nt):
        send_squares(o).wait_send()


def hidden_call(nt, x, squares, gate_weight, up_weight):
    tokens, width = x.shape
    units = gate_weight.shape[1]
    rows = tokens // nt
    chunks = units // COLS
    sem = pltpu.SemaphoreType.DMA((chunks,))
    return pl.pallas_call(
        functools.partial(hidden_kernel, nt),
        out_shape=jax.ShapeDtypeStruct((tokens, units), jnp.bfloat16),
        in_specs=[pl.BlockSpec(memory_space=pltpu.VMEM)] * 2
        + [pl.BlockSpec(memory_space=pl.ANY)] * 2,
        out_specs=pl.BlockSpec(memory_space=pltpu.VMEM),
        scratch_shapes=[
            pltpu.VMEM((width, units), jnp.bfloat16),
            pltpu.VMEM((width, units), jnp.bfloat16),
            pltpu.VMEM((nt, rows, 2 * COLS), jnp.float32),
            pltpu.VMEM((chunks, nt // 2, rows, 2 * COLS), jnp.float32),
            pltpu.VMEM((chunks, nt // 2, rows, 2 * COLS), jnp.bfloat16),
            pltpu.VMEM((chunks, nt // 2, rows, 2 * COLS), jnp.bfloat16),
            pltpu.VMEM((chunks, rows, 2 * COLS), jnp.bfloat16),
            pltpu.VMEM((chunks, rows, 2 * COLS), jnp.bfloat16),
            pltpu.VMEM((chunks, nt, rows, COLS), jnp.bfloat16),
            pltpu.VMEM((nt - 1, rows, 128), jnp.float32),
            sem,
            sem,
            pltpu.SemaphoreType.DMA((nt - 1,)),
            pltpu.SemaphoreType.DMA((nt - 1,)),
        ]
        + [sem] * 10,
        compiler_params=pltpu.CompilerParams(
            collective_id=1, has_side_effects=True, vmem_limit_bytes=VMEM_LIMIT
        ),
    )(x, squares, gate_weight, up_weight)


def down_kernel(
    nc, hidden, w_hbm, base, out, w, part, b0, b1, b2, b3, q0, q1, q2, q3, wsem
):
    ci, ti = lax.axis_index("ctx"), lax.axis_index("tp")
    rows = base.shape[0]
    chunks = part.shape[0]

    def get(k):
        return pltpu.make_async_copy(w_hbm.at[:, columns(k)], w.at[:, columns(k)], wsem.at[k])

    for k in range(chunks):
        get(k).start()
    greet([(lax.rem(ci + o, nc), ti) for o in range(1, nc)])

    def compute(k):
        get(k).wait()
        part[k] = jnp.dot(
            hidden[...], w[:, columns(k)], preferred_element_type=jnp.float32
        ).reshape(nc, rows, COLS)

    def finish(k, own):
        out[:, columns(k)] = (part[k, own] + base[:, columns(k)].astype(jnp.float32)).astype(
            jnp.bfloat16
        )

    line_sum(ci, ti, nc, True, compute, finish, part, (b0, b1, b2, b3), (q0, q1, q2, q3))


def down_call(nc, hidden, down_weight, attended):
    rows, width = attended.shape
    depth = down_weight.shape[0]
    chunks = width // COLS
    return pl.pallas_call(
        functools.partial(down_kernel, nc),
        out_shape=jax.ShapeDtypeStruct((rows, width), jnp.bfloat16),
        in_specs=[
            pl.BlockSpec(memory_space=pltpu.VMEM),
            pl.BlockSpec(memory_space=pl.ANY),
            pl.BlockSpec(memory_space=pltpu.VMEM),
        ],
        out_specs=pl.BlockSpec(memory_space=pltpu.VMEM),
        scratch_shapes=[
            pltpu.VMEM((depth, width), jnp.bfloat16),
            pltpu.VMEM((chunks, nc, rows, COLS), jnp.float32),
        ]
        + [pltpu.VMEM((chunks, nc, rows, COLS), jnp.bfloat16)] * 4
        + [pltpu.SemaphoreType.DMA((chunks, nc))] * 4
        + [pltpu.SemaphoreType.DMA((chunks,))],
        compiler_params=pltpu.CompilerParams(
            collective_id=2, has_side_effects=True, vmem_limit_bytes=VMEM_LIMIT
        ),
    )(hidden, down_weight, attended)


def kernels_fit(nc, nt, rows, width, depth, units):
    tokens = nc * rows
    attend = 2 * depth * width + 2 * tokens * depth + 16 * tokens * width
    middle = 4 * width * units + 20 * tokens * units + 2 * tokens * width
    down = 2 * units * width + 2 * tokens * units + 14 * tokens * width
    return (
        nt == 4
        and nc == nt
        and rows % (16 * nt) == 0
        and width % COLS == 0
        and units % COLS == 0
        and max(attend, middle, down) < VMEM_LIMIT - 2 * 1024 * 1024
    )


def on_device(
    residual,
    latent,
    queries,
    lengths,
    value_weight,
    output_weight,
    norm_gain,
    gate_weight,
    up_weight,
    down_weight,
):
    row_count = residual.shape[0]
    ctx_place = lax.axis_index("ctx")
    local_heads = value_weight.shape[1] // VHEAD
    own_index = ctx_place * row_count + jnp.arange(row_count, dtype=jnp.int32)
    own_trace, own_position = trace_info(own_index, lengths)
    rotated_keys = rope_keys(latent, own_position, LAT)
    rotated_queries = rope_queries(
        queries.reshape(row_count, local_heads, LAT + ROPE), own_position, LAT
    )
    last_query = ctx_place * row_count + row_count - 1
    start_state = (
        jnp.full((local_heads, row_count), masked_score, jnp.float32),
        jnp.zeros((local_heads, row_count), jnp.float32),
        jnp.zeros((local_heads, row_count, LAT), jnp.float32),
    )
    nc, nt = lax.axis_size("ctx"), lax.axis_size("tp")
    fits = kernels_fit(
        nc, nt, row_count, residual.shape[1], output_weight.shape[0], gate_weight.shape[1]
    )
    if fits and row_count % LANES == 0 and latent.shape[0] % 32 == 0:
        key_piece = keys_call(nc, nt, rotated_keys)
    else:
        key_piece = lax.all_gather(rotated_keys, "ctx", axis=1, tiled=True)
    key_index = jnp.arange(key_piece.shape[1], dtype=jnp.int32)
    key_trace, _ = trace_info(key_index, lengths)
    folded = lax.cond(
        jnp.int32(0) <= last_query,
        lambda held: score_rows(
            held, rotated_queries, own_index, own_trace, key_piece, key_index, key_trace
        ),
        lambda held: held,
        start_state,
    )
    row_top, row_total, mixed_sum = folded
    mixed_latent = (mixed_sum / row_total[:, :, None]).astype(jnp.bfloat16)
    heads_out = (
        jnp.einsum(
            "hql,lhd->qhd",
            mixed_latent,
            value_weight.reshape(LAT, local_heads, VHEAD),
            preferred_element_type=jnp.float32,
        )
        .astype(jnp.bfloat16)
        .reshape(row_count, local_heads * VHEAD)
    )
    if fits:
        attended, gained, squares = attend_call(
            nc, nt, heads_out, output_weight, residual, norm_gain
        )
        squares = squares.reshape(nt, nc * row_count // nt, LANES)
        hidden = hidden_call(nt, gained, squares, gate_weight, up_weight)
        return (attended, down_call(nc, hidden, down_weight, attended))
    all_heads = lax.all_gather(heads_out, "tp", axis=1, tiled=True)
    head_block = lax.all_to_all(all_heads, "ctx", split_axis=1, concat_axis=0, tiled=True)
    head_sum = lax.psum_scatter(
        jnp.dot(head_block, output_weight, preferred_element_type=jnp.float32).astype(jnp.bfloat16),
        "ctx",
        scatter_dimension=0,
        tiled=True,
    ).astype(jnp.float32)
    attended = (residual.astype(jnp.float32) + head_sum).astype(jnp.bfloat16)
    attended_float = attended.astype(jnp.float32)
    squares = lax.psum(jnp.sum(attended_float * attended_float, axis=1), "tp")
    inverse_rms = lax.rsqrt(squares / D + norm_eps)
    scaled = (attended_float * inverse_rms[:, None] * norm_gain[None, :]).astype(jnp.bfloat16)
    scaled_all = lax.all_gather(scaled, "ctx", axis=0, tiled=True)
    unit_count = gate_weight.shape[1]
    gate_up = jnp.concatenate([gate_weight, up_weight], axis=1)
    summed = lax.psum_scatter(
        jnp.dot(scaled_all, gate_up, preferred_element_type=jnp.float32).astype(jnp.bfloat16),
        "tp",
        scatter_dimension=0,
        tiled=True,
    ).astype(jnp.float32)
    hidden_share = (jax.nn.silu(summed[:, :unit_count]) * summed[:, unit_count:]).astype(
        jnp.bfloat16
    )
    hidden_all = lax.all_gather(hidden_share, "tp", axis=0, tiled=True)
    down_sum = lax.psum_scatter(
        jnp.dot(hidden_all, down_weight, preferred_element_type=jnp.float32).astype(jnp.bfloat16),
        "ctx",
        scatter_dimension=0,
        tiled=True,
    ).astype(jnp.float32)
    layer_out = (attended_float + down_sum).astype(jnp.bfloat16)
    return (attended, layer_out)


def solution(mesh):
    in_specs = (
        P(("grp", "ctx"), "tp"),
        P(None, ("grp", "ctx")),
        P(("grp", "ctx"), "tp"),
        P("grp"),
        P(None, "tp"),
        P("ctx", "tp"),
        P("tp"),
        P("tp", "ctx"),
        P("tp", "ctx"),
        P("ctx", "tp"),
    )
    out_specs = (P(("grp", "ctx"), "tp"), P(("grp", "ctx"), "tp"))
    return jax.shard_map(
        on_device, mesh=mesh, in_specs=in_specs, out_specs=out_specs, check_vma=False
    )
```

```python
import functools

import jax
import jax.numpy as jnp
from jax import lax
from jax.experimental import pallas as pl
from jax.experimental.pallas import tpu as pltpu
from jax.sharding import PartitionSpec as P

D = 7168
LAT = 512
ROPE = 64
VHEAD = 128


score_scale = 192.0 ** (-0.5)
rope_base = 10000.0
norm_eps = 1e-06
masked_score = -1e30


def rope_freqs(half_width):
    return rope_base ** (-jnp.arange(half_width, dtype=jnp.float32) / half_width)


def trace_info(token_index, lengths):
    trace_ends = jnp.cumsum(lengths)
    starts = trace_ends - lengths
    trace_ids = jnp.sum((token_index[:, None] >= trace_ends[None, :]).astype(jnp.int32), axis=1)
    member = trace_ids[:, None] == jnp.arange(lengths.shape[0], dtype=jnp.int32)[None, :]
    pos_shift = jnp.sum(jnp.where(member, (0 - starts)[None, :], 0), axis=1)
    return (trace_ids, token_index + pos_shift)


def rope_keys(latent, positions, latent_width):
    values = latent.astype(jnp.float32)
    half_width = (values.shape[0] - latent_width) // 2
    angles = rope_freqs(half_width)[:, None] * positions.astype(jnp.float32)[None, :]
    first_half = values[latent_width : latent_width + half_width]
    second_half = values[latent_width + half_width :]
    cosine = jnp.cos(angles)
    sine_value = jnp.sin(angles)
    return jnp.concatenate(
        [
            values[:latent_width],
            first_half * cosine - second_half * sine_value,
            first_half * sine_value + second_half * cosine,
        ],
        axis=0,
    ).astype(jnp.bfloat16)


def rope_queries(queries, positions, latent_width):
    values = queries.astype(jnp.float32)
    half_width = (values.shape[2] - latent_width) // 2
    angles = positions.astype(jnp.float32)[:, None] * rope_freqs(half_width)[None, :]
    cosine = jnp.cos(angles)[:, None, :]
    sine_value = jnp.sin(angles)[:, None, :]
    first_half = values[:, :, latent_width : latent_width + half_width]
    second_half = values[:, :, latent_width + half_width :]
    return jnp.concatenate(
        [
            values[:, :, :latent_width],
            first_half * cosine - second_half * sine_value,
            first_half * sine_value + second_half * cosine,
        ],
        axis=2,
    ).astype(jnp.bfloat16)


def score_rows(state_carry, query_block, block_index, block_trace, key_piece, key_index, key_trace):
    row_top, row_total, mixed_sum = state_carry
    allowed = (key_trace[None, :] == block_trace[:, None]) & (
        key_index[None, :] <= block_index[:, None]
    )
    scores = (
        jnp.einsum("qhe,ek->hqk", query_block, key_piece, preferred_element_type=jnp.float32)
        * score_scale
    )
    scores = jnp.where(allowed[None], scores, masked_score)
    new_top = jnp.maximum(row_top, jnp.max(scores, axis=2))
    exponent = jnp.where(allowed[None], jnp.exp(scores - new_top[:, :, None]), 0.0)
    row_total = jnp.sum(exponent, axis=2)
    mixed_sum = jnp.einsum(
        "hqk,lk->hql",
        exponent.astype(jnp.bfloat16),
        key_piece[:LAT],
        preferred_element_type=jnp.float32,
    )
    return (new_top, row_total, mixed_sum)


MESH = pl.DeviceIdType.MESH
COLS = 256
LANES = 128
VMEM_LIMIT = 60 * 1024 * 1024


def remote(src, dst, send_sem, recv_sem, ctx, tp):
    return pltpu.make_async_remote_copy(
        src_ref=src,
        dst_ref=dst,
        send_sem=send_sem,
        recv_sem=recv_sem,
        device_id={"ctx": ctx, "tp": tp},
        device_id_type=MESH,
    )


def greet(partners):
    barrier = pltpu.get_barrier_semaphore()
    for ctx, tp in partners:
        pl.semaphore_signal(
            barrier, inc=1, device_id={"ctx": ctx, "tp": tp}, device_id_type=MESH
        )
    pl.semaphore_wait(barrier, len(partners))


def greet_all(ci, ti, nc, nt):
    flat = ci * nt + ti
    partners = []
    for offset in range(1, nc * nt):
        other = lax.rem(flat + offset, nc * nt)
        partners.append((other // nt, lax.rem(other, nt)))
    greet(partners)


def line_sum(ci, ti, nc, scatter, compute, finish, part, bufs, sems):
    send_r, send_l, recv_r, recv_l = bufs
    out_r, out_l, in_r, in_l = sems
    chunks, blocks = part.shape[0], part.shape[1]

    def right(k, d):
        return remote(
            send_r.at[k, d], recv_r.at[k, d], out_r.at[k, d], in_r.at[k, d],
            lax.rem(ci + 1, nc), ti,
        )

    def left(k, d):
        return remote(
            send_l.at[k, d], recv_l.at[k, d], out_l.at[k, d], in_l.at[k, d],
            lax.rem(ci + nc - 1, nc), ti,
        )

    def forward(k, copy, send, recv, is_first, wanted):
        for d in range(blocks):

            @pl.when(wanted(d))
            def _():
                @pl.when(is_first)
                def _():
                    send[k, d] = part[k, d].astype(jnp.bfloat16)

                @pl.when(jnp.logical_not(is_first))
                def _():
                    copy(k, d).wait_recv()
                    send[k, d] = (part[k, d] + recv[k, d].astype(jnp.float32)).astype(
                        jnp.bfloat16
                    )

                copy(k, d).start()

    go_right = (lambda d: d > ci) if scatter else (lambda d: ci < nc - 1)
    go_left = (lambda d: d < ci) if scatter else (lambda d: ci > 0)

    def step(s, carry):
        @pl.when(s < chunks)
        def _():
            compute(s)

        r = s - ci

        @pl.when((ci < nc - 1) & (r >= 0) & (r < chunks))
        def _():
            forward(r, right, send_r, recv_r, ci == 0, go_right)

        l = s - (nc - 1 - ci)

        @pl.when((ci > 0) & (l >= 0) & (l < chunks))
        def _():
            forward(l, left, send_l, recv_l, ci == nc - 1, go_left)

        return carry

    lax.fori_loop(0, chunks + nc - 1, step, 0)

    def last(k, carry):
        for own in [ci] if scatter else range(blocks):

            @pl.when(ci > 0)
            def _():
                if scatter:
                    right(k, own).wait_recv()
                else:

                    @pl.when(ci == nc - 1)
                    def _():
                        right(k, own).wait_recv()

                part[k, own] += recv_r[k, own].astype(jnp.float32)

            @pl.when(ci < nc - 1)
            def _():
                if scatter:
                    left(k, own).wait_recv()
                else:

                    @pl.when(ci == 0)
                    def _():
                        left(k, own).wait_recv()

                part[k, own] += recv_l[k, own].astype(jnp.float32)

        finish(k)
        return carry

    lax.fori_loop(0, chunks, last, 0)

    def drain(k, carry):
        for d in range(blocks):

            @pl.when(go_right(d))
            def _():
                right(k, d).wait_send()

            @pl.when(go_left(d))
            def _():
                left(k, d).wait_send()

        return carry

    lax.fori_loop(0, chunks, drain, 0)


def columns(k):
    return pl.ds(pl.multiple_of(k * COLS, COLS), COLS)


def keys_kernel(nc, nt, keys, out, held, s1, r1, s2, r2):
    ci, ti = lax.axis_index("ctx"), lax.axis_index("tp")
    height, width = keys.shape
    half = height // 2
    core = lax.rem(ti, 2)
    mate = ti + 1 - 2 * core
    greet([(lax.rem(ci + o, nc), ti) for o in range(1, nc)] + [(ci, mate)])

    def place(c):
        return pl.ds(pl.multiple_of(c * width, width), width)

    def share(which):
        return pl.ds(pl.multiple_of(which * half, half), half)

    def across(o):
        return remote(
            keys.at[share(core), :], held.at[share(core), place(ci)], s1.at[o - 1],
            r1.at[o - 1], lax.rem(ci + o, nc), ti,
        )

    def to_mate(o, which):
        spot = held.at[share(which), place(lax.rem(ci + nc - o, nc))]
        return remote(spot, spot, s2.at[o - 1], r2.at[o - 1], ci, mate)

    def arrived(o):
        spot = held.at[share(core), place(lax.rem(ci + nc - o, nc))]
        return remote(spot, spot, s1.at[o - 1], r1.at[o - 1], ci, mate)

    for o in range(1, nc):
        across(o).start()
    held[:, place(ci)] = keys[...]
    for o in range(1, nc):
        arrived(o).wait_recv()
        to_mate(o, core).start()
    for o in range(1, nc):
        to_mate(o, 1 - core).wait_recv()
    for o in range(1, nc):
        across(o).wait_send()
        to_mate(o, core).wait_send()
    out[...] = held[...]


def keys_call(nc, nt, keys):
    height, width = keys.shape
    sem = pltpu.SemaphoreType.DMA((nc - 1,))
    return pl.pallas_call(
        functools.partial(keys_kernel, nc, nt),
        out_shape=jax.ShapeDtypeStruct((height, nc * width), jnp.bfloat16),
        in_specs=[pl.BlockSpec(memory_space=pltpu.VMEM)],
        out_specs=pl.BlockSpec(memory_space=pltpu.VMEM),
        scratch_shapes=[pltpu.VMEM((height, nc * width), jnp.bfloat16)] + [sem] * 4,
        compiler_params=pltpu.CompilerParams(collective_id=3, has_side_effects=True),
    )(keys)


def attend_kernel(
    nc, nt, ho, w_hbm, res, gain, att, x, squares, h, w, part, b0, b1, b2, b3,
    q0, q1, q2, q3, wsem, lsem, s1, r1, s2, r2, s3, r3, s4, r4,
):
    ci, ti = lax.axis_index("ctx"), lax.axis_index("tp")
    rows = res.shape[0]
    fetch = pltpu.make_async_copy(w_hbm, w, wsem)
    fetch.start()
    greet_all(ci, ti, nc, nt)
    mate = ti + 1 - 2 * lax.rem(ti, 2)
    across = lax.rem(ti + 2, nt)
    mine = ci == ti

    def first(q, c):
        return remote(ho.at[q], h.at[c, q], s1.at[q], r1.at[c], ti, q)

    for q in range(nt):
        to_self = mine & (ti == q)

        @pl.when(to_self)
        def _():
            pltpu.make_async_copy(ho.at[q], h.at[ci, q], lsem).start()

        @pl.when(jnp.logical_not(to_self))
        def _():
            first(q, ci).start()

    def to_mate(c):
        return remote(h.at[c, ti], h.at[c, ti], s2.at[c], r2.at[c], ci, mate)

    def to_across(c):
        return remote(h.at[c, ti], h.at[c, ti], s3.at[c], r3.at[c], ci, across)

    def relay(c):
        return remote(h.at[c, across], h.at[c, across], s4.at[c], r4.at[c], ci, mate)

    for c in range(nc):
        from_self = mine & (ci == c)

        @pl.when(from_self)
        def _():
            pltpu.make_async_copy(ho.at[ti], h.at[c, ti], lsem).wait()

        @pl.when(jnp.logical_not(from_self))
        def _():
            remote(ho.at[ti], h.at[c, ti], s1.at[ti], r1.at[c], ci, mate).wait_recv()

        to_across(c).start()
        to_mate(c).start()
    for c in range(nc):
        remote(h.at[c, across], h.at[c, across], s3.at[c], r3.at[c], ci, across).wait_recv()
        relay(c).start()
    far = lax.rem(mate + 2, nt)
    for c in range(nc):
        remote(h.at[c, mate], h.at[c, mate], s2.at[c], r2.at[c], ci, mate).wait_recv()
        remote(h.at[c, far], h.at[c, far], s4.at[c], r4.at[c], ci, mate).wait_recv()
    fetch.wait()

    def compute(k):
        part[k] = jnp.dot(
            h[...].reshape(nc * rows, h.shape[3]),
            w[:, columns(k)],
            preferred_element_type=jnp.float32,
        ).reshape(nc, rows, COLS)
        part[k, ci] += res[:, columns(k)].astype(jnp.float32)

    squares[...] = jnp.zeros_like(squares)

    def finish(k):
        total = part[k].reshape(nc * rows, COLS).astype(jnp.bfloat16).astype(jnp.float32)
        x[:, columns(k)] = (total * gain[:, columns(k)]).astype(jnp.bfloat16)
        power = total * total
        squares[...] += sum(power[:, i : i + LANES] for i in range(0, COLS, LANES))
        att[:, columns(k)] = part[k, ci].astype(jnp.bfloat16)

    line_sum(ci, ti, nc, False, compute, finish, part, (b0, b1, b2, b3), (q0, q1, q2, q3))
    for q in range(nt):

        @pl.when(jnp.logical_not(mine & (ti == q)))
        def _():
            first(q, ci).wait_send()

    for c in range(nc):
        to_mate(c).wait_send()
        to_across(c).wait_send()
        relay(c).wait_send()


def attend_call(nc, nt, heads_out, output_weight, residual, gain):
    rows, width = residual.shape
    depth = output_weight.shape[0]
    chunks = width // COLS
    buf = pltpu.VMEM((chunks, nc, rows, COLS), jnp.bfloat16)
    sem = pltpu.SemaphoreType.DMA((chunks, nc))
    return pl.pallas_call(
        functools.partial(attend_kernel, nc, nt),
        out_shape=(
            jax.ShapeDtypeStruct((rows, width), jnp.bfloat16),
            jax.ShapeDtypeStruct((nc * rows, width), jnp.bfloat16),
            jax.ShapeDtypeStruct((nc * rows, LANES), jnp.float32),
        ),
        in_specs=[
            pl.BlockSpec(memory_space=pltpu.VMEM),
            pl.BlockSpec(memory_space=pl.ANY),
            pl.BlockSpec(memory_space=pltpu.VMEM),
            pl.BlockSpec(memory_space=pltpu.VMEM),
        ],
        out_specs=[pl.BlockSpec(memory_space=pltpu.VMEM)] * 3,
        scratch_shapes=[
            pltpu.VMEM((nc, nt, rows // nt, depth), jnp.bfloat16),
            pltpu.VMEM((depth, width), jnp.bfloat16),
            pltpu.VMEM((chunks, nc, rows, COLS), jnp.float32),
        ]
        + [buf] * 4
        + [sem] * 4
        + [pltpu.SemaphoreType.DMA, pltpu.SemaphoreType.DMA]
        + [pltpu.SemaphoreType.DMA((nt,)), pltpu.SemaphoreType.DMA((nc,))]
        + [pltpu.SemaphoreType.DMA((nc,))] * 6,
        compiler_params=pltpu.CompilerParams(
            collective_id=0, has_side_effects=True, vmem_limit_bytes=VMEM_LIMIT
        ),
    )(heads_out.reshape(nt, rows // nt, depth), output_weight, residual, gain[None, :])


def hidden_kernel(
    nt, x, squares, gate_hbm, up_hbm, out, gate, up, g_all, kept, sa, ra, sb, rb, hb, sq,
    gsem, usem, sqs, sqr, sas, sar, sbs, sbr, hxs, hxr, hcs, hcr, hfs, hfr,
):
    ci, ti = lax.axis_index("ctx"), lax.axis_index("tp")
    chunks = gsem.shape[0]
    rows = squares.shape[1]

    def get(k, hbm, held, sem):
        return pltpu.make_async_copy(hbm.at[:, columns(k)], held.at[:, columns(k)], sem.at[k])

    for k in range(chunks):
        get(k, gate_hbm, gate, gsem).start()
        get(k, up_hbm, up, usem).start()
    greet([(ci, lax.rem(ti + o, nt)) for o in range(1, nt)])
    mate = ti + 1 - 2 * lax.rem(ti, 2)
    across = lax.rem(ti + 2, nt)
    far = lax.rem(mate + 2, nt)
    core = lax.rem(ti, 2)
    side = ti // 2

    def send_squares(o):
        other = lax.rem(ti + o, nt)
        return remote(
            squares.at[other], sq.at[o - 1], sqs.at[o - 1], sqr.at[o - 1], ci, other
        )

    for o in range(1, nt):
        send_squares(o).start()

    def to_mate(k):
        return remote(sa.at[k], ra.at[k], sas.at[k], sar.at[k], ci, mate)

    def to_across(k):
        return remote(sb.at[k], rb.at[k], sbs.at[k], sbr.at[k], ci, across)

    def hid(k, owner, send, recv, target):
        return remote(hb.at[k, owner], hb.at[k, owner], send.at[k], recv.at[k], ci, target)

    total = squares[ti]
    for o in range(1, nt):
        send_squares(o).wait_recv()
        total = total + sq[o - 1]
    mean = jnp.sum(total, axis=1, keepdims=True) / D
    sq[0] = jnp.broadcast_to(lax.rsqrt(mean + norm_eps), total.shape)

    def step(s, carry):
        @pl.when(s < chunks)
        def _():
            get(s, gate_hbm, gate, gsem).wait()
            get(s, up_hbm, up, usem).wait()
            for place, held in ((0, gate), (1, up)):
                g_all[:, :, place * COLS : (place + 1) * COLS] = jnp.dot(
                    x[...], held[:, columns(s)], preferred_element_type=jnp.float32
                ).reshape(nt, rows, COLS)
            for i in range(nt // 2):
                sa[s, i] = g_all[2 * i + 1 - core].astype(jnp.bfloat16)
                kept[s, i] = g_all[2 * i + core]
            to_mate(s).start()

        a = s - 1

        @pl.when((a >= 0) & (a < chunks))
        def _():
            to_mate(a).wait_recv()
            sb[a] = (kept[a, 1 - side] + ra[a, 1 - side].astype(jnp.float32)).astype(
                jnp.bfloat16
            )
            to_across(a).start()
            kept[a, side] += ra[a, side].astype(jnp.float32)

        b = s - 3

        @pl.when((b >= 0) & (b < chunks))
        def _():
            to_across(b).wait_recv()
            inverse = sq[0][:, :1]
            summed = (kept[b, side] + rb[b].astype(jnp.float32)) * inverse
            hb[b, ti] = (jax.nn.silu(summed[:, :COLS]) * summed[:, COLS:]).astype(jnp.bfloat16)
            hid(b, ti, hxs, hxr, across).start()
            hid(b, ti, hcs, hcr, mate).start()

        c = s - 5

        @pl.when((c >= 0) & (c < chunks))
        def _():
            hid(c, across, hxs, hxr, across).wait_recv()
            hid(c, across, hfs, hfr, mate).start()

        return carry

    lax.fori_loop(0, chunks + 5, step, 0)

    def last(k, carry):
        hid(k, mate, hcs, hcr, mate).wait_recv()
        hid(k, far, hfs, hfr, mate).wait_recv()
        out[:, columns(k)] = hb[k].reshape(nt * rows, COLS)
        to_mate(k).wait_send()
        to_across(k).wait_send()
        hid(k, ti, hxs, hxr, across).wait_send()
        hid(k, ti, hcs, hcr, mate).wait_send()
        hid(k, across, hfs, hfr, mate).wait_send()
        return carry

    lax.fori_loop(0, chunks, last, 0)
    for o in range(1, nt):
        send_squares(o).wait_send()


def hidden_call(nt, x, squares, gate_weight, up_weight):
    tokens, width = x.shape
    units = gate_weight.shape[1]
    rows = tokens // nt
    chunks = units // COLS
    sem = pltpu.SemaphoreType.DMA((chunks,))
    return pl.pallas_call(
        functools.partial(hidden_kernel, nt),
        out_shape=jax.ShapeDtypeStruct((tokens, units), jnp.bfloat16),
        in_specs=[pl.BlockSpec(memory_space=pltpu.VMEM)] * 2
        + [pl.BlockSpec(memory_space=pl.ANY)] * 2,
        out_specs=pl.BlockSpec(memory_space=pltpu.VMEM),
        scratch_shapes=[
            pltpu.VMEM((width, units), jnp.bfloat16),
            pltpu.VMEM((width, units), jnp.bfloat16),
            pltpu.VMEM((nt, rows, 2 * COLS), jnp.float32),
            pltpu.VMEM((chunks, nt // 2, rows, 2 * COLS), jnp.float32),
            pltpu.VMEM((chunks, nt // 2, rows, 2 * COLS), jnp.bfloat16),
            pltpu.VMEM((chunks, nt // 2, rows, 2 * COLS), jnp.bfloat16),
            pltpu.VMEM((chunks, rows, 2 * COLS), jnp.bfloat16),
            pltpu.VMEM((chunks, rows, 2 * COLS), jnp.bfloat16),
            pltpu.VMEM((chunks, nt, rows, COLS), jnp.bfloat16),
            pltpu.VMEM((nt - 1, rows, 128), jnp.float32),
            sem,
            sem,
            pltpu.SemaphoreType.DMA((nt - 1,)),
            pltpu.SemaphoreType.DMA((nt - 1,)),
        ]
        + [sem] * 10,
        compiler_params=pltpu.CompilerParams(
            collective_id=1, has_side_effects=True, vmem_limit_bytes=VMEM_LIMIT
        ),
    )(x, squares, gate_weight, up_weight)


def down_kernel(
    nc, hidden, w_hbm, base, out, w, part, b0, b1, b2, b3, q0, q1, q2, q3, wsem
):
    ci, ti = lax.axis_index("ctx"), lax.axis_index("tp")
    rows = base.shape[0]
    chunks = part.shape[0]

    def get(k):
        return pltpu.make_async_copy(w_hbm.at[:, columns(k)], w.at[:, columns(k)], wsem.at[k])

    for k in range(chunks):
        get(k).start()
    greet([(lax.rem(ci + o, nc), ti) for o in range(1, nc)])

    def compute(k):
        get(k).wait()
        part[k] = jnp.dot(
            hidden[...], w[:, columns(k)], preferred_element_type=jnp.float32
        ).reshape(nc, rows, COLS)

    def finish(k):
        out[:, columns(k)] = (part[k, ci] + base[:, columns(k)].astype(jnp.float32)).astype(
            jnp.bfloat16
        )

    line_sum(ci, ti, nc, True, compute, finish, part, (b0, b1, b2, b3), (q0, q1, q2, q3))


def down_call(nc, hidden, down_weight, attended):
    rows, width = attended.shape
    depth = down_weight.shape[0]
    chunks = width // COLS
    return pl.pallas_call(
        functools.partial(down_kernel, nc),
        out_shape=jax.ShapeDtypeStruct((rows, width), jnp.bfloat16),
        in_specs=[
            pl.BlockSpec(memory_space=pltpu.VMEM),
            pl.BlockSpec(memory_space=pl.ANY),
            pl.BlockSpec(memory_space=pltpu.VMEM),
        ],
        out_specs=pl.BlockSpec(memory_space=pltpu.VMEM),
        scratch_shapes=[
            pltpu.VMEM((depth, width), jnp.bfloat16),
            pltpu.VMEM((chunks, nc, rows, COLS), jnp.float32),
        ]
        + [pltpu.VMEM((chunks, nc, rows, COLS), jnp.bfloat16)] * 4
        + [pltpu.SemaphoreType.DMA((chunks, nc))] * 4
        + [pltpu.SemaphoreType.DMA((chunks,))],
        compiler_params=pltpu.CompilerParams(
            collective_id=2, has_side_effects=True, vmem_limit_bytes=VMEM_LIMIT
        ),
    )(hidden, down_weight, attended)


def kernels_fit(nc, nt, rows, width, depth, units):
    tokens = nc * rows
    attend = 2 * depth * width + 2 * tokens * depth + 16 * tokens * width
    middle = 4 * width * units + 20 * tokens * units + 2 * tokens * width
    down = 2 * units * width + 2 * tokens * units + 14 * tokens * width
    return (
        nt == 4
        and nc == nt
        and rows % (16 * nt) == 0
        and width % COLS == 0
        and units % COLS == 0
        and max(attend, middle, down) < VMEM_LIMIT - 2 * 1024 * 1024
    )


def on_device(
    residual,
    latent,
    queries,
    lengths,
    value_weight,
    output_weight,
    norm_gain,
    gate_weight,
    up_weight,
    down_weight,
):
    row_count = residual.shape[0]
    ctx_place = lax.axis_index("ctx")
    local_heads = value_weight.shape[1] // VHEAD
    own_index = ctx_place * row_count + jnp.arange(row_count, dtype=jnp.int32)
    own_trace, own_position = trace_info(own_index, lengths)
    rotated_keys = rope_keys(latent, own_position, LAT)
    rotated_queries = rope_queries(
        queries.reshape(row_count, local_heads, LAT + ROPE), own_position, LAT
    )
    last_query = ctx_place * row_count + row_count - 1
    start_state = (
        jnp.full((local_heads, row_count), masked_score, jnp.float32),
        jnp.zeros((local_heads, row_count), jnp.float32),
        jnp.zeros((local_heads, row_count, LAT), jnp.float32),
    )
    nc, nt = lax.axis_size("ctx"), lax.axis_size("tp")
    fits = kernels_fit(
        nc, nt, row_count, residual.shape[1], output_weight.shape[0], gate_weight.shape[1]
    )
    if fits and row_count % LANES == 0 and latent.shape[0] % 32 == 0:
        key_piece = keys_call(nc, nt, rotated_keys)
    else:
        key_piece = lax.all_gather(rotated_keys, "ctx", axis=1, tiled=True)
    key_index = jnp.arange(key_piece.shape[1], dtype=jnp.int32)
    key_trace, _ = trace_info(key_index, lengths)
    folded = lax.cond(
        jnp.int32(0) <= last_query,
        lambda held: score_rows(
            held, rotated_queries, own_index, own_trace, key_piece, key_index, key_trace
        ),
        lambda held: held,
        start_state,
    )
    row_top, row_total, mixed_sum = folded
    mixed_latent = (mixed_sum / row_total[:, :, None]).astype(jnp.bfloat16)
    heads_out = (
        jnp.einsum(
            "hql,lhd->qhd",
            mixed_latent,
            value_weight.reshape(LAT, local_heads, VHEAD),
            preferred_element_type=jnp.float32,
        )
        .astype(jnp.bfloat16)
        .reshape(row_count, local_heads * VHEAD)
    )
    if fits:
        attended, gained, squares = attend_call(
            nc, nt, heads_out, output_weight, residual, norm_gain
        )
        squares = squares.reshape(nt, nc * row_count // nt, LANES)
        hidden = hidden_call(nt, gained, squares, gate_weight, up_weight)
        return (attended, down_call(nc, hidden, down_weight, attended))
    all_heads = lax.all_gather(heads_out, "tp", axis=1, tiled=True)
    head_block = lax.all_to_all(all_heads, "ctx", split_axis=1, concat_axis=0, tiled=True)
    head_sum = lax.psum_scatter(
        jnp.dot(head_block, output_weight, preferred_element_type=jnp.float32).astype(jnp.bfloat16),
        "ctx",
        scatter_dimension=0,
        tiled=True,
    ).astype(jnp.float32)
    attended = (residual.astype(jnp.float32) + head_sum).astype(jnp.bfloat16)
    attended_float = attended.astype(jnp.float32)
    squares = lax.psum(jnp.sum(attended_float * attended_float, axis=1), "tp")
    inverse_rms = lax.rsqrt(squares / D + norm_eps)
    scaled = (attended_float * inverse_rms[:, None] * norm_gain[None, :]).astype(jnp.bfloat16)
    scaled_all = lax.all_gather(scaled, "ctx", axis=0, tiled=True)
    unit_count = gate_weight.shape[1]
    gate_up = jnp.concatenate([gate_weight, up_weight], axis=1)
    summed = lax.psum_scatter(
        jnp.dot(scaled_all, gate_up, preferred_element_type=jnp.float32).astype(jnp.bfloat16),
        "tp",
        scatter_dimension=0,
        tiled=True,
    ).astype(jnp.float32)
    hidden_share = (jax.nn.silu(summed[:, :unit_count]) * summed[:, unit_count:]).astype(
        jnp.bfloat16
    )
    hidden_all = lax.all_gather(hidden_share, "tp", axis=0, tiled=True)
    down_sum = lax.psum_scatter(
        jnp.dot(hidden_all, down_weight, preferred_element_type=jnp.float32).astype(jnp.bfloat16),
        "ctx",
        scatter_dimension=0,
        tiled=True,
    ).astype(jnp.float32)
    layer_out = (attended_float + down_sum).astype(jnp.bfloat16)
    return (attended, layer_out)


def solution(mesh):
    in_specs = (
        P(("grp", "ctx"), "tp"),
        P(None, ("grp", "ctx")),
        P(("grp", "ctx"), "tp"),
        P("grp"),
        P(None, "tp"),
        P("ctx", "tp"),
        P("tp"),
        P("tp", "ctx"),
        P("tp", "ctx"),
        P("ctx", "tp"),
    )
    out_specs = (P(("grp", "ctx"), "tp"), P(("grp", "ctx"), "tp"))
    return jax.shard_map(
        on_device, mesh=mesh, in_specs=in_specs, out_specs=out_specs, check_vma=False
    )
```
